32 devices in a mesh: tgt: 8 (over z, core), sup: 4 (over y, x).
Axes of the slice: x: 2, y: 2, z: 4, core: 2. Of those that a mesh axis runs over, the one named last changes fastest.
Arguments:
- target_pool: float32 [512, 3, 1024], P('tgt'), may hold values from -6 to 6
- target_index: int32 [64], P('tgt'), may hold values from 0 to 511, as said below
- target_labels: int32 [64], P('tgt'), may hold values from 0 to 99
- dual_weights: float32 [128, 100], P('sup'), may hold values from -0.5 to 0.5
- support_images: float32 [128, 3, 1024], P(('sup', 'tgt')), may hold values from -6 to 6
Outputs:
- residual: float32 [64, 100], P('tgt')
- support_grad: float32 [128, 3, 1024], P(('sup', 'tgt'))
The draws below stay inside these ranges and needn't reach their ends.
Inputs may be any that keep to these rules, and one draw needn't show every extreme that they name: `target_index`: for each j, the targets 8 * j to 8 * (j + 1) - 1 name distinct candidates among 64 * j to 64 * (j + 1) - 1.
All inputs are finite; a program needn't handle non-finite values.
Results may differ from the reference program's by a relative error of at most 0.0003.
Values sent between devices are 32-bit elements; how exact they have to be, the bound alone decides.
A program may use at most 64 MiB of HBM per device.

```python
import math
import jax
import jax.numpy as jnp
from jax import lax

CHANNELS = 3
SIDE = 32
CLASSES = 100
LAYERS = 3
TGT_DEV = 8
POOL_DEV = 64
PIXELS = 1024
TARGETS = 64
SUPPORT = 128
POOL = 512


def draw_target_index(key, part):
    blocks = TARGETS // TGT_DEV
    block_keys = jax.random.split(key, blocks)
    block_ids = jnp.arange(blocks)

    def one_block(block_key, block_id):
        first_key, second_key, third_key = jax.random.split(block_key, 3)
        drawn = jax.random.permutation(first_key, POOL_DEV)[:TGT_DEV]
        others = jax.random.permutation(second_key, POOL_DEV - 1)[:TGT_DEV - 1]
        with_low = jnp.concatenate([others + 1, jnp.zeros((1,), jnp.int32)])
        with_high = jnp.concatenate([others, jnp.full((1,), POOL_DEV - 1, jnp.int32)])
        picked = jnp.where(block_id == 0, with_low, jnp.where(block_id == blocks - 1, with_high, drawn.astype(jnp.int32)))
        order = jax.random.permutation(third_key, TGT_DEV)
        return jnp.take(picked, order)
    chosen = jax.vmap(one_block)(block_keys, block_ids)
    offsets = (block_ids * POOL_DEV)[:, None]
    return (chosen + offsets).reshape(-1).astype(jnp.int32)


def place_ends(array, own_key, low, high):
    index_at = [jax.random.randint(jax.random.fold_in(own_key, axis), (), 0, length) for axis, length in enumerate(array.shape)]
    longest = array.shape.index(max(array.shape))
    beside = index_at[:longest] + [(index_at[longest] + 1) % array.shape[longest]] + index_at[longest + 1:]
    return array.at[tuple(index_at)].set(low).at[tuple(beside)].set(high)


def block_scale(rng, shape, cuts, least, top_value):
    def one(axis_at, blocks):
        steps = jax.random.uniform(jax.random.fold_in(jax.random.fold_in(rng, 6), axis_at), (blocks,), jnp.float32, least / len(cuts), top_value / len(cuts))
        return jnp.repeat(jnp.exp(steps), shape[axis_at] // blocks).reshape((-1,) + (1,) * (len(shape) - axis_at - 1))

    gain = one(*cuts[0])
    for cut in cuts[1:]:
        gain = gain * one(*cut)
    return gain


def noise(key, dims, width, bound, pieces=(), kind=jnp.bfloat16):
    values = jax.random.normal(key, dims, jnp.float32) * width
    if len(pieces) > 0:
        values = block_scale(key, dims, pieces, -0.22, 0.18) * values
    return jnp.clip(values, min=-bound, max=bound).astype(kind)


def setup_inputs(seed: int = 0) -> dict:
    seeds = jax.random.split(jax.random.key(seed), 6)
    target_pool = noise(seeds[0], (POOL, CHANNELS, PIXELS), 1.0, 6.0, ((0, 8),), jnp.float32)
    target_index = draw_target_index(jax.random.fold_in(seeds[5], 71), 0)
    target_labels = place_ends(jax.random.randint(seeds[2], (TARGETS,), 0, CLASSES), jax.random.fold_in(seeds[2], 1), 0, CLASSES - 1).astype(jnp.int32)
    dual_weights = noise(seeds[3], (SUPPORT, CLASSES), SUPPORT ** -0.5, 0.5, ((0, 4),), jnp.float32)
    support_images = noise(seeds[4], (SUPPORT, CHANNELS, PIXELS), 1.0, 6.0, ((0, 32),), jnp.float32)
    return {"target_pool": target_pool, "target_index": target_index, "target_labels": target_labels, "dual_weights": dual_weights, "support_images": support_images}


bias_variance = 0.01

def box_filter(pixel_map):
    column = jnp.arange(PIXELS) % SIDE
    zero_column = jnp.zeros(pixel_map.shape[:-1] + (1,), pixel_map.dtype)
    shifted_right = jnp.concatenate([zero_column, pixel_map[..., :-1]], axis=-1)
    shifted_left = jnp.concatenate([pixel_map[..., 1:], zero_column], axis=-1)
    across = pixel_map + jnp.where(column > 0, shifted_right, 0.0) + jnp.where(column < SIDE - 1, shifted_left, 0.0)
    zero_row = jnp.zeros(pixel_map.shape[:-1] + (SIDE,), pixel_map.dtype)
    shifted_down = jnp.concatenate([zero_row, across[..., :-SIDE]], axis=-1)
    shifted_up = jnp.concatenate([across[..., SIDE:], zero_row], axis=-1)
    return (across + shifted_down + shifted_up) / 9.0

def self_maps(images):
    energy = images[:, 0] * images[:, 0]
    for channel in range(1, CHANNELS):
        energy = energy + images[:, channel] * images[:, channel]
    current = box_filter(energy / CHANNELS) + bias_variance
    levels = [current]
    for layer_index in range(1, LAYERS):
        current = box_filter(current) + bias_variance
        levels.append(current)
    return levels

def rectified(cross, target_level, support_level):
    spread = jnp.sqrt(target_level * support_level - cross * cross)
    polar_angle = jnp.arctan2(spread, cross)
    return ((spread + (math.pi - polar_angle) * cross) / math.pi, spread, polar_angle)

def cross_forward(targets, support, target_levels, support_levels):
    inner_sum = targets[:, None, 0] * support[None, :, 0]
    for channel in range(1, CHANNELS):
        inner_sum = inner_sum + targets[:, None, channel] * support[None, :, channel]
    cross = box_filter(inner_sum / CHANNELS) + bias_variance
    saved_maps = []
    output_map = cross
    for layer_index in range(LAYERS):
        output_map, spread, polar_angle = rectified(cross, target_levels[layer_index][:, None], support_levels[layer_index][None])
        saved_maps.append((spread, polar_angle))
        if layer_index + 1 < LAYERS:
            cross = box_filter(output_map) + bias_variance
    return (lax.optimization_barrier(jnp.mean(output_map, axis=-1)), saved_maps)

def cross_backward(weight, saved_maps, targets, support, support_levels):
    upstream = weight[:, :, None]
    level_grad = None
    for layer_index in range(LAYERS - 1, -1, -1):
        spread, polar_angle = saved_maps[layer_index]
        level_term = lax.optimization_barrier(jnp.sum(upstream * spread, axis=0)) / (2.0 * math.pi * support_levels[layer_index])
        level_grad = level_term if level_grad is None else level_term + box_filter(level_grad)
        upstream = box_filter(upstream * (math.pi - polar_angle) / math.pi)
    energy_grad = box_filter(level_grad) / CHANNELS
    channel_grads = []
    for channel in range(CHANNELS):
        carried = lax.optimization_barrier(jnp.sum(upstream * targets[:, None, channel], axis=0)) / CHANNELS
        channel_grads.append(carried + 2.0 * support[:, channel] * energy_grad)
    return jnp.stack(channel_grads, axis=1)

def reference(target_pool, target_index, target_labels, dual_weights, support_images):
    targets = jnp.take(target_pool, target_index, axis=0)
    onehot = (target_labels[:, None] == jnp.arange(CLASSES)[None, :]).astype(jnp.float32)
    support_levels = self_maps(support_images)
    blocks = targets.reshape((TARGETS // TGT_DEV, TGT_DEV) + targets.shape[1:])

    def block_kernel(block):
        kernel_rows, saved_maps = cross_forward(block, support_images, self_maps(block), support_levels)
        return kernel_rows
    kernel = lax.map(block_kernel, blocks).reshape(TARGETS, SUPPORT)
    predicted = jnp.dot(kernel, dual_weights, precision=lax.Precision.HIGHEST, preferred_element_type=jnp.float32)
    residual = predicted - onehot
    weight = jnp.dot(residual, dual_weights.T, precision=lax.Precision.HIGHEST, preferred_element_type=jnp.float32)
    weight_blocks = weight.reshape(TARGETS // TGT_DEV, TGT_DEV, SUPPORT)

    def block_grad(total, pair_block):
        block, block_weight = pair_block
        kernel_rows, saved_maps = cross_forward(block, support_images, self_maps(block), support_levels)
        return (total + cross_backward(block_weight, saved_maps, block, support_images, support_levels), None)
    support_grad, unused = lax.scan(block_grad, jnp.zeros(support_images.shape, jnp.float32), (blocks, weight_blocks))
    return (residual, support_grad)
```

```python
import functools
import math

import jax
import jax.numpy as jnp
from jax import lax
from jax.experimental import pallas as pl
from jax.experimental.pallas import tpu as pltpu
from jax.sharding import PartitionSpec as P

CHANNELS = 3
SIDE = 32
CLASSES = 100
LAYERS = 3
PIXELS = 1024
BETA = 0.01
PACK = 4
SUB = 8
LANES = 128
MESH = pl.DeviceIdType.MESH
HIGH = lax.Precision.HIGHEST
ACOS = (
    1.5707963050,
    -0.2145988016,
    0.0889789874,
    -0.0501743046,
    0.0308918810,
    -0.0170881256,
    0.0066700901,
    -0.0012624911,
)


def masks():
    lane = lax.broadcasted_iota(jnp.int32, (SUB, LANES), 1)
    row = lax.broadcasted_iota(jnp.int32, (SUB, LANES), 0)
    column = lane % SIDE
    return (column > 0, column < SIDE - 1, row > 0, row < SUB - 1, lane // SIDE)


def box_sum(maps, mask):
    right, left, down, up, _ = mask
    axis = maps[0].ndim - 1

    def across(v):
        return (
            v
            + jnp.where(right, pltpu.roll(v, 1, axis), 0.0)
            + jnp.where(left, pltpu.roll(v, LANES - 1, axis), 0.0)
        )

    before = jnp.where(down, pltpu.roll(maps[3], 1, axis - 1), 0.0)
    after = jnp.where(up, pltpu.roll(maps[0], SUB - 1, axis - 1), 0.0)
    low = maps[0] + maps[1]
    high = maps[2] + maps[3]
    return [across(v) for v in (before + low, low + maps[2], maps[1] + high, high + after)]


def interleave(images, mask):
    group = mask[4]
    out = []
    for k in range(PACK):
        total = None
        for m in range(PACK):
            shift = ((m - k) * SIDE) % LANES
            moved = images[m] if shift == 0 else pltpu.roll(images[m], shift, 1)
            total = moved if total is None else jnp.where(group == m, moved, total)
        out.append(total)
    return out


def replicate(image, mask):
    group = mask[4]
    out = []
    rolled = [image] + [pltpu.roll(image, SIDE * s, 1) for s in range(1, PACK)]
    for k in range(PACK):
        total = None
        for m in range(PACK):
            moved = rolled[(m - k) % PACK]
            total = moved if total is None else jnp.where(group == m, moved, total)
        out.append(total)
    return out


def levels_of(images, mask):
    energy = []
    for k in range(PACK):
        total = images[0][k] * images[0][k]
        for channel in range(1, CHANNELS):
            total = total + images[channel][k] * images[channel][k]
        energy.append(total * (1.0 / CHANNELS))
    levels = []
    current = energy
    for _ in range(LAYERS):
        current = [v * (1.0 / 9.0) + BETA for v in box_sum(current, mask)]
        levels.append(current)
    return levels


def kernel(
    nt, ns, own_t, own_s,
    index_ref, label_ref, pool_ref, dual_ref, support_ref,
    residual_ref, grad_ref,
    tbuf, dbuf, kbuf, srep, sroot, tlev, amp, ang, ksum, wexp, accl, accc, pred, flat,
    plane_send, plane_recv, part_send, part_recv, dual_send, dual_recv, k_send, k_recv,
):
    ti = lax.axis_index("tgt")
    si = lax.axis_index("sup")
    chips = nt // 2
    chip = ti // 2
    core = ti % 2
    ndev = nt * ns
    me = si * nt + ti
    groups_own = own_t // PACK
    groups = nt * groups_own
    images = groups_own * CHANNELS * PACK
    targets = nt * own_t
    mask = masks()

    barrier = pltpu.get_barrier_semaphore()

    def greet(step, carry):
        other = lax.rem(me + step, ndev)
        pl.semaphore_signal(
            barrier, inc=1, device_id=(lax.rem(other, nt), other // nt), device_id_type=MESH
        )
        return carry

    lax.fori_loop(1, ndev, greet, 0)

    pool = pool_ref.shape[1] * SUB
    picks = [lax.rem(index_ref[t], pool) for t in range(own_t)]
    for gl in range(groups_own):
        for channel in range(CHANNELS):
            natural = [
                pool_ref[channel, at // SUB, :, pl.ds(at % SUB, 1), :].reshape(SUB, LANES)
                for at in picks[gl * PACK : (gl + 1) * PACK]
            ]
            phases = interleave(natural, mask)
            for k in range(PACK):
                tbuf[ti, (gl * CHANNELS + channel) * PACK + k] = phases[k]
    row = lax.broadcasted_iota(jnp.int32, (SUB, LANES), 0)
    lane = lax.broadcasted_iota(jnp.int32, (SUB, LANES), 1)
    label = jnp.zeros((SUB, LANES), jnp.int32)
    for r in range(own_t):
        label = jnp.where(row == r, label_ref[r], label)
    own_onehot = jnp.where(label == lane, 1.0, 0.0).astype(jnp.float32)
    tbuf[ti, images] = own_onehot
    dbuf[si] = dual_ref[...]

    pl.semaphore_wait(barrier, ndev - 1)

    def plane_copy(target_chip):
        return pltpu.make_async_remote_copy(
            src_ref=tbuf.at[ti],
            dst_ref=tbuf.at[ti],
            send_sem=plane_send.at[target_chip],
            recv_sem=plane_recv.at[chip],
            device_id=(target_chip * 2 + core, si),
            device_id_type=MESH,
        )

    def plane_arrival(source_chip):
        return pltpu.make_async_remote_copy(
            src_ref=tbuf.at[source_chip * 2 + core],
            dst_ref=tbuf.at[source_chip * 2 + core],
            send_sem=plane_send.at[source_chip],
            recv_sem=plane_recv.at[source_chip],
            device_id=(source_chip * 2 + core, si),
            device_id_type=MESH,
        )

    def part_copy(p):
        return pltpu.make_async_remote_copy(
            src_ref=tbuf.at[p * 2 + core],
            dst_ref=tbuf.at[p * 2 + core],
            send_sem=part_send.at[p],
            recv_sem=part_recv.at[p],
            device_id=(chip * 2 + 1 - core, si),
            device_id_type=MESH,
        )

    def part_arrival(p):
        return pltpu.make_async_remote_copy(
            src_ref=tbuf.at[p * 2 + 1 - core],
            dst_ref=tbuf.at[p * 2 + 1 - core],
            send_sem=part_send.at[p],
            recv_sem=part_recv.at[p],
            device_id=(chip * 2 + 1 - core, si),
            device_id_type=MESH,
        )

    def dual_copy(s):
        return pltpu.make_async_remote_copy(
            src_ref=dbuf.at[si],
            dst_ref=dbuf.at[si],
            send_sem=dual_send.at[s],
            recv_sem=dual_recv.at[si],
            device_id=(ti, s),
            device_id_type=MESH,
        )

    def dual_arrival(s):
        return pltpu.make_async_remote_copy(
            src_ref=dbuf.at[s],
            dst_ref=dbuf.at[s],
            send_sem=dual_send.at[s],
            recv_sem=dual_recv.at[s],
            device_id=(ti, s),
            device_id_type=MESH,
        )

    def k_copy(d):
        return pltpu.make_async_remote_copy(
            src_ref=kbuf.at[me],
            dst_ref=kbuf.at[me],
            send_sem=k_send.at[d],
            recv_sem=k_recv.at[me],
            device_id=(lax.rem(d, nt), d // nt),
            device_id_type=MESH,
        )

    def k_arrival(d):
        return pltpu.make_async_remote_copy(
            src_ref=kbuf.at[d],
            dst_ref=kbuf.at[d],
            send_sem=k_send.at[d],
            recv_sem=k_recv.at[d],
            device_id=(lax.rem(d, nt), d // nt),
            device_id_type=MESH,
        )

    for h in range(1, chips):
        @pl.when(chip >= h)
        def _():
            plane_copy(chip - h).start()

        @pl.when(chip + h < chips)
        def _():
            plane_copy(chip + h).start()

    def send_dual(step, carry):
        dual_copy(lax.rem(si + step, ns)).start()
        return carry

    lax.fori_loop(1, ns, send_dual, 0)

    for m in range(own_s):
        reps = []
        for channel in range(CHANNELS):
            phases = replicate(support_ref[channel, :, m, :], mask)
            reps.append(phases)
            for k in range(PACK):
                srep[channel, k, m] = phases[k]
        levels = levels_of(reps, mask)
        for layer in range(LAYERS):
            for k in range(PACK):
                inverse = lax.rsqrt(levels[layer][k])
                sroot[layer, 0, k, m] = inverse * (1.0 / 9.0**layer)
                sroot[layer, 1, k, m] = levels[layer][k] * inverse * (9.0**layer / math.pi)

    def group_forward(owner, gl):
        g = owner * groups_own + gl
        image = [
            [tbuf[owner, (gl * CHANNELS + channel) * PACK + k] for k in range(PACK)]
            for channel in range(CHANNELS)
        ]
        levels = levels_of(image, mask)
        for layer in range(LAYERS):
            for k in range(PACK):
                inverse = lax.rsqrt(levels[layer][k])
                tlev[layer, 0, k] = inverse
                tlev[layer, 1, k] = levels[layer][k] * inverse
        current = []
        for k in range(PACK):
            total = image[0][k][None] * srep[0, k]
            for channel in range(1, CHANNELS):
                total = total + image[channel][k][None] * srep[channel, k]
            current.append(total)
        cross = [v * (1.0 / 27.0) + BETA for v in box_sum(current, mask)]
        for layer in range(LAYERS):
            mapped = []
            for k in range(PACK):
                x = cross[k] * (tlev[layer, 0, k][None] * sroot[layer, 0, k])
                size = jnp.abs(x)
                gap = jnp.maximum(1.0 - size, 1e-20)
                rest = 1.0 + size
                half = gap * lax.rsqrt(gap)
                poly = size * (ACOS[7] / math.pi) + ACOS[6] / math.pi
                for term in ACOS[5::-1]:
                    poly = poly * size + term / math.pi
                near = half * poly
                slope = jnp.where(x >= 0.0, 1.0 - near, near)
                sine = half * (rest * lax.rsqrt(rest))
                scaled = sine * tlev[layer, 1, k][None]
                amp[g, layer, k] = scaled
                ang[g, layer, k] = slope
                mapped.append(scaled * sroot[layer, 1, k] + slope * cross[k])
            if layer + 1 < LAYERS:
                cross = [v + BETA * 9.0 ** (layer + 1) for v in box_sum(mapped, mask)]
        total = (mapped[0] + mapped[1]) + (mapped[2] + mapped[3])
        ksum[:, pl.ds(g, 1), :] = jnp.sum(total, axis=1, keepdims=True)

    def block_forward(owner):
        def one(gl, carry):
            group_forward(owner, gl)
            return carry

        lax.fori_loop(0, groups_own, one, 0)

    def order(n):
        both = jnp.minimum(chip, chips - 1 - chip)
        h = (n + 1) // 2
        two_sided = jnp.where(n % 2 == 1, chip - h, chip + h)
        far = n - both
        one_sided = jnp.where(chip <= chips - 1 - chip, chip + far, chip - far)
        return jnp.where(n <= 2 * both, two_sided, one_sided)

    def visit(n, carry):
        p = order(n)

        @pl.when(n > 0)
        def _():
            plane_arrival(p).wait_recv()

        part_copy(p).start()
        block_forward(p * 2 + core)
        part_arrival(p).wait_recv()
        block_forward(p * 2 + 1 - core)
        return carry

    lax.fori_loop(0, chips, visit, 0)

    spread_row = lax.broadcasted_iota(jnp.int32, (targets, LANES), 0)
    spread_lane = lax.broadcasted_iota(jnp.int32, (targets, LANES), 1)
    spread = jnp.where(spread_row % PACK == spread_lane // SIDE, 1.0, 0.0).astype(jnp.float32)
    keep_g = lax.broadcasted_iota(jnp.int32, (groups, targets), 0)
    keep_t = lax.broadcasted_iota(jnp.int32, (groups, targets), 1)
    keep = jnp.where(keep_t // PACK == keep_g, 1.0, 0.0).astype(jnp.float32)
    nt_dims = (((1,), (1,)), ((), ()))
    lane_sums = lax.dot_general(
        ksum[...].reshape(own_s * groups, LANES), spread, nt_dims,
        precision=HIGH, preferred_element_type=jnp.float32,
    ) * (1.0 / (PIXELS * 9.0 ** (LAYERS - 1)))
    picked = jnp.sum(lane_sums.reshape(own_s, groups, targets) * keep[None], axis=1)
    kbuf[me] = picked

    def send_k(step, carry):
        k_copy(lax.rem(me + step, ndev)).start()
        return carry

    lax.fori_loop(1, ndev, send_k, 0)

    def take_dual(step, carry):
        dual_arrival(lax.rem(si + step, ns)).wait_recv()
        return carry

    lax.fori_loop(1, ns, take_dual, 0)
    duals = dbuf[...].reshape(ns * dual_ref.shape[0], CLASSES)
    own_duals = dual_ref[pl.ds(ti * own_s, own_s), :]
    gram = lax.dot_general(
        own_duals, duals, nt_dims, precision=HIGH, preferred_element_type=jnp.float32
    )
    onehot = tbuf[:, images].reshape(targets, LANES)[:, :CLASSES]
    offset = lax.dot_general(
        own_duals, onehot, nt_dims, precision=HIGH, preferred_element_type=jnp.float32
    )
    accl[...] = jnp.zeros_like(accl)
    accc[...] = jnp.zeros_like(accc)

    def take_k(step, carry):
        k_arrival(lax.rem(me + step, ndev)).wait_recv()
        return carry

    lax.fori_loop(1, ndev, take_k, 0)
    columns = jnp.concatenate([kbuf[d] for d in range(ndev)], axis=0)
    weight = jnp.dot(gram, columns, precision=HIGH, preferred_element_type=jnp.float32) - offset
    wide = (weight[:, None, :] * keep[None]).reshape(own_s * groups, targets)
    wexp[...] = jnp.dot(
        wide, spread, precision=HIGH, preferred_element_type=jnp.float32
    ).reshape(own_s, groups, LANES)

    def block_backward(owner, carry):
        level_terms = [[None] * PACK for _ in range(LAYERS)]
        channel_terms = [[None] * PACK for _ in range(CHANNELS)]

        def add(table, at, k, value):
            table[at][k] = value if table[at][k] is None else table[at][k] + value

        for gl in range(groups_own):
            g = owner * groups_own + gl
            upstream = [jnp.broadcast_to(wexp[:, pl.ds(g, 1), :], (own_s, SUB, LANES))] * PACK
            for layer in range(LAYERS - 1, -1, -1):
                passed = []
                for k in range(PACK):
                    add(level_terms, layer, k, upstream[k] * amp[g, layer, k])
                    passed.append(upstream[k] * ang[g, layer, k])
                upstream = box_sum(passed, mask)
            for channel in range(CHANNELS):
                for k in range(PACK):
                    image = tbuf[owner, (gl * CHANNELS + channel) * PACK + k]
                    add(channel_terms, channel, k, upstream[k] * image[None])
        for layer in range(LAYERS):
            for k in range(PACK):
                accl[layer, k] += level_terms[layer][k]
        for channel in range(CHANNELS):
            for k in range(PACK):
                accc[channel, k] += channel_terms[channel][k]
        return carry

    lax.fori_loop(0, nt, block_backward, 0)

    def over_images(v):
        v = v + pltpu.roll(v, 2 * SIDE, 2)
        return v + pltpu.roll(v, SIDE, 2)

    level_grad = None
    for layer in range(LAYERS - 1, -1, -1):
        scale = 9.0**layer / (2.0 * math.pi * 9.0 ** (LAYERS - 1 - layer))
        term = [
            over_images(accl[layer, k]) * (sroot[layer, 0, k] * scale) for k in range(PACK)
        ]
        if level_grad is not None:
            carried = box_sum(level_grad, mask)
            term = [t + c * (1.0 / 9.0) for t, c in zip(term, carried)]
        level_grad = term
    energy = [v * (2.0 / (9.0 * CHANNELS)) for v in box_sum(level_grad, mask)]
    for channel in range(CHANNELS):
        natural = None
        for k in range(PACK):
            value = over_images(accc[channel, k]) * (1.0 / (CHANNELS * 9.0**LAYERS))
            value = value + srep[channel, k] * energy[k]
            natural = value if natural is None else jnp.where(mask[4] == k, value, natural)
        flat[...] = natural
        for s in range(SUB):
            grad_ref[channel, s] = flat[:, s, :]

    pred[...] = jnp.dot(columns.T, duals, precision=HIGH, preferred_element_type=jnp.float32)
    residual_ref[...] = pred[pl.ds(ti * own_t, own_t), :] - own_onehot[:own_t, :CLASSES]

    for p in range(chips):
        @pl.when(chip != p)
        def _():
            plane_copy(p).wait_send()

        part_copy(p).wait_send()

    def drain_dual(step, carry):
        dual_copy(lax.rem(si + step, ns)).wait_send()
        return carry

    lax.fori_loop(1, ns, drain_dual, 0)

    def drain_k(step, carry):
        k_copy(lax.rem(me + step, ndev)).wait_send()
        return carry

    lax.fori_loop(1, ndev, drain_k, 0)


def shards(nt, ns, target_pool, target_index, target_labels, dual_weights, support_images):
    own_t = target_index.shape[0]
    own_s = support_images.shape[0]
    groups = nt * own_t // PACK
    images = own_t * CHANNELS
    chips = nt // 2
    ndev = nt * ns
    f32 = jnp.float32
    vmem = pl.BlockSpec(memory_space=pltpu.VMEM)
    smem = pl.BlockSpec(memory_space=pltpu.SMEM)
    dma = pltpu.SemaphoreType.DMA
    tile = (SUB, LANES)
    residual, grad = pl.pallas_call(
        functools.partial(kernel, nt, ns, own_t, own_s),
        out_shape=(
            jax.ShapeDtypeStruct((own_t, CLASSES), f32),
            jax.ShapeDtypeStruct((CHANNELS, SUB, own_s, LANES), f32),
        ),
        in_specs=[smem, smem, vmem, vmem, vmem],
        out_specs=(vmem, vmem),
        scratch_shapes=[
            pltpu.VMEM((nt, images + 1) + tile, f32),
            pltpu.VMEM((ns,) + dual_weights.shape, f32),
            pltpu.VMEM((ndev, own_s, nt * own_t), f32),
            pltpu.VMEM((CHANNELS, PACK, own_s) + tile, f32),
            pltpu.VMEM((LAYERS, 2, PACK, own_s) + tile, f32),
            pltpu.VMEM((LAYERS, 2, PACK) + tile, f32),
            pltpu.VMEM((groups, LAYERS, PACK, own_s) + tile, f32),
            pltpu.VMEM((groups, LAYERS, PACK, own_s) + tile, f32),
            pltpu.VMEM((own_s, groups, LANES), f32),
            pltpu.VMEM((own_s, groups, LANES), f32),
            pltpu.VMEM((LAYERS, PACK, own_s) + tile, f32),
            pltpu.VMEM((CHANNELS, PACK, own_s) + tile, f32),
            pltpu.VMEM((nt * own_t, CLASSES), f32),
            pltpu.VMEM((own_s,) + tile, f32),
            dma((chips,)),
            dma((chips,)),
            dma((chips,)),
            dma((chips,)),
            dma((ns,)),
            dma((ns,)),
            dma((ndev,)),
            dma((ndev,)),
        ],
        compiler_params=pltpu.CompilerParams(collective_id=0, has_side_effects=True),
    )(
        target_index,
        target_labels,
        target_pool.reshape(-1, SUB, CHANNELS, SUB, LANES).transpose(2, 0, 3, 1, 4),
        dual_weights,
        support_images.reshape(own_s, CHANNELS, SUB, LANES).transpose(1, 2, 0, 3),
    )
    return (residual, grad.transpose(2, 0, 1, 3).reshape(support_images.shape))


def solution(mesh):
    in_specs = (
        P("tgt", None, None),
        P("tgt"),
        P("tgt"),
        P("sup", None),
        P(("sup", "tgt"), None, None),
    )
    out_specs = (P("tgt", None), P(("sup", "tgt"), None, None))
    body = functools.partial(shards, mesh.shape["tgt"], mesh.shape["sup"])
    return jax.shard_map(body, mesh=mesh, in_specs=in_specs, out_specs=out_specs, check_vma=False)
```

```python
import functools
import math

import jax
import jax.numpy as jnp
from jax import lax
from jax.experimental import pallas as pl
from jax.experimental.pallas import tpu as pltpu
from jax.sharding import PartitionSpec as P

CHANNELS = 3
SIDE = 32
CLASSES = 100
LAYERS = 3
PIXELS = 1024
BETA = 0.01
PACK = 4
SUB = 8
LANES = 128
MESH = pl.DeviceIdType.MESH
HIGH = lax.Precision.HIGHEST
ACOS = (
    1.5707963050,
    -0.2145988016,
    0.0889789874,
    -0.0501743046,
    0.0308918810,
    -0.0170881256,
    0.0066700901,
    -0.0012624911,
)


def masks():
    lane = lax.broadcasted_iota(jnp.int32, (SUB, LANES), 1)
    row = lax.broadcasted_iota(jnp.int32, (SUB, LANES), 0)
    column = lane % SIDE
    return (column > 0, column < SIDE - 1, row > 0, row < SUB - 1, lane // SIDE)


def box_sum(maps, mask):
    right, left, down, up, _ = mask
    axis = maps[0].ndim - 1

    def across(v):
        return (
            v
            + jnp.where(right, pltpu.roll(v, 1, axis), 0.0)
            + jnp.where(left, pltpu.roll(v, LANES - 1, axis), 0.0)
        )

    before = jnp.where(down, pltpu.roll(maps[3], 1, axis - 1), 0.0)
    after = jnp.where(up, pltpu.roll(maps[0], SUB - 1, axis - 1), 0.0)
    low = maps[0] + maps[1]
    high = maps[2] + maps[3]
    return [across(v) for v in (before + low, low + maps[2], maps[1] + high, high + after)]


def interleave(images, mask):
    group = mask[4]
    out = []
    for k in range(PACK):
        total = None
        for m in range(PACK):
            shift = ((m - k) * SIDE) % LANES
            moved = images[m] if shift == 0 else pltpu.roll(images[m], shift, 1)
            total = moved if total is None else jnp.where(group == m, moved, total)
        out.append(total)
    return out


def replicate(image, mask):
    group = mask[4]
    out = []
    rolled = [image] + [pltpu.roll(image, SIDE * s, 1) for s in range(1, PACK)]
    for k in range(PACK):
        total = None
        for m in range(PACK):
            moved = rolled[(m - k) % PACK]
            total = moved if total is None else jnp.where(group == m, moved, total)
        out.append(total)
    return out


def levels_of(images, mask):
    energy = []
    for k in range(PACK):
        total = images[0][k] * images[0][k]
        for channel in range(1, CHANNELS):
            total = total + images[channel][k] * images[channel][k]
        energy.append(total * (1.0 / CHANNELS))
    levels = []
    current = energy
    for _ in range(LAYERS):
        current = [v * (1.0 / 9.0) + BETA for v in box_sum(current, mask)]
        levels.append(current)
    return levels


def kernel(
    nt, ns, own_t, own_s,
    index_ref, label_ref, pool_ref, dual_ref, support_ref,
    residual_ref, grad_ref,
    tbuf, dbuf, kbuf, srep, sroot, tlev, amp, ang, ksum, wexp, accl, accc, pred, flat,
    plane_send, plane_recv, part_send, part_recv, dual_send, dual_recv, k_send, k_recv,
):
    ti = lax.axis_index("tgt")
    si = lax.axis_index("sup")
    chips = nt // 2
    chip = ti // 2
    core = ti % 2
    ndev = nt * ns
    me = si * nt + ti
    groups_own = own_t // PACK
    groups = nt * groups_own
    images = groups_own * CHANNELS * PACK
    targets = nt * own_t
    mask = masks()

    barrier = pltpu.get_barrier_semaphore()

    def others(action):
        for s in range(ns):
            for t in range(nt):
                pl.when((si != s) | (ti != t))(functools.partial(action, t, s))

    def greet(t, s):
        pl.semaphore_signal(barrier, inc=1, device_id=(t, s), device_id_type=MESH)

    others(greet)

    pool = pool_ref.shape[1] * SUB
    picks = [lax.rem(index_ref[t], pool) for t in range(own_t)]
    for gl in range(groups_own):
        for channel in range(CHANNELS):
            natural = [
                pool_ref[channel, at // SUB, :, pl.ds(at % SUB, 1), :].reshape(SUB, LANES)
                for at in picks[gl * PACK : (gl + 1) * PACK]
            ]
            phases = interleave(natural, mask)
            for k in range(PACK):
                tbuf[ti, (gl * CHANNELS + channel) * PACK + k] = phases[k]
    row = lax.broadcasted_iota(jnp.int32, (SUB, LANES), 0)
    lane = lax.broadcasted_iota(jnp.int32, (SUB, LANES), 1)
    label = jnp.zeros((SUB, LANES), jnp.int32)
    for r in range(own_t):
        label = jnp.where(row == r, label_ref[r], label)
    own_onehot = jnp.where(label == lane, 1.0, 0.0).astype(jnp.float32)
    tbuf[ti, images] = own_onehot
    dbuf[si] = dual_ref[...]

    pl.semaphore_wait(barrier, ndev - 1)

    def chunk(owner, gl):
        first = gl * CHANNELS * PACK
        last = images + 1 if gl == groups_own - 1 else first + CHANNELS * PACK
        return tbuf.at[owner, pl.ds(first, last - first)]

    def plane_copy(source_chip, gl, way, target_chip):
        part = chunk(source_chip * 2 + core, gl)
        return pltpu.make_async_remote_copy(
            src_ref=part,
            dst_ref=part,
            send_sem=plane_send.at[way, source_chip, gl],
            recv_sem=plane_recv.at[source_chip, gl],
            device_id=(target_chip * 2 + core, si),
            device_id_type=MESH,
        )

    def part_copy(p, gl, side):
        part = chunk(p * 2 + side, gl)
        return pltpu.make_async_remote_copy(
            src_ref=part,
            dst_ref=part,
            send_sem=part_send.at[p, gl],
            recv_sem=part_recv.at[p, gl],
            device_id=(chip * 2 + 1 - core, si),
            device_id_type=MESH,
        )

    def handle(h, gl):
        for way in range(2):
            step = 1 - 2 * way
            source = chip - step * h
            onward = chip + step

            @pl.when((source >= 0) & (source < chips))
            def _():
                plane_copy(source, gl, way, source).wait_recv()

                @pl.when((onward >= 0) & (onward < chips))
                def _():
                    plane_copy(source, gl, way, onward).start()

                part_copy(source, gl, core).start()

    def dual_copy(s):
        return pltpu.make_async_remote_copy(
            src_ref=dbuf.at[si],
            dst_ref=dbuf.at[si],
            send_sem=dual_send.at[s],
            recv_sem=dual_recv.at[si],
            device_id=(ti, s),
            device_id_type=MESH,
        )

    def dual_arrival(s):
        return pltpu.make_async_remote_copy(
            src_ref=dbuf.at[s],
            dst_ref=dbuf.at[s],
            send_sem=dual_send.at[s],
            recv_sem=dual_recv.at[s],
            device_id=(ti, s),
            device_id_type=MESH,
        )

    def k_copy(t, s):
        return pltpu.make_async_remote_copy(
            src_ref=kbuf.at[me],
            dst_ref=kbuf.at[me],
            send_sem=k_send,
            recv_sem=k_recv,
            device_id=(t, s),
            device_id_type=MESH,
        )

    def k_all():
        others_slots = kbuf.at[pl.ds(0, ndev - 1)]
        return pltpu.make_async_remote_copy(
            src_ref=others_slots,
            dst_ref=others_slots,
            send_sem=k_send,
            recv_sem=k_recv,
            device_id=(1 - core + chip * 2, si),
            device_id_type=MESH,
        )

    for gl in range(groups_own):
        for way in range(2):
            onward = chip + 1 - 2 * way

            @pl.when((onward >= 0) & (onward < chips))
            def _():
                plane_copy(chip, gl, way, onward).start()

        part_copy(chip, gl, core).start()

    def send_dual(step, carry):
        dual_copy(lax.rem(si + step, ns)).start()
        return carry

    lax.fori_loop(1, ns, send_dual, 0)

    for m in range(own_s):
        reps = []
        for channel in range(CHANNELS):
            phases = replicate(support_ref[channel, :, m, :], mask)
            reps.append(phases)
            for k in range(PACK):
                srep[channel, k, m] = phases[k]
        levels = levels_of(reps, mask)
        for layer in range(LAYERS):
            for k in range(PACK):
                inverse = lax.rsqrt(levels[layer][k])
                sroot[layer, 0, k, m] = inverse * (1.0 / 9.0**layer)
                sroot[layer, 1, k, m] = levels[layer][k] * inverse * (9.0**layer / math.pi)

    def group_forward(owner, gl):
        g = owner * groups_own + gl
        image = [
            [tbuf[owner, (gl * CHANNELS + channel) * PACK + k] for k in range(PACK)]
            for channel in range(CHANNELS)
        ]
        levels = levels_of(image, mask)
        for layer in range(LAYERS):
            for k in range(PACK):
                inverse = lax.rsqrt(levels[layer][k])
                tlev[layer, 0, k] = inverse
                tlev[layer, 1, k] = levels[layer][k] * inverse
        current = []
        for k in range(PACK):
            total = image[0][k][None] * srep[0, k]
            for channel in range(1, CHANNELS):
                total = total + image[channel][k][None] * srep[channel, k]
            current.append(total)
        cross = [v * (1.0 / 27.0) + BETA for v in box_sum(current, mask)]
        for layer in range(LAYERS):
            mapped = []
            for k in range(PACK):
                x = cross[k] * (tlev[layer, 0, k][None] * sroot[layer, 0, k])
                size = jnp.abs(x)
                gap = jnp.maximum(1.0 - size, 1e-20)
                rest = 1.0 + size
                half = gap * lax.rsqrt(gap)
                poly = size * (ACOS[7] / math.pi) + ACOS[6] / math.pi
                for term in ACOS[5::-1]:
                    poly = poly * size + term / math.pi
                near = half * poly
                slope = jnp.where(x >= 0.0, 1.0 - near, near)
                sine = half * (rest * lax.rsqrt(rest))
                scaled = sine * tlev[layer, 1, k][None]
                amp[g, layer, k] = scaled
                ang[g, layer, k] = slope
                mapped.append(scaled * sroot[layer, 1, k] + slope * cross[k])
            if layer + 1 < LAYERS:
                cross = [v + BETA * 9.0 ** (layer + 1) for v in box_sum(mapped, mask)]
        total = (mapped[0] + mapped[1]) + (mapped[2] + mapped[3])
        ksum[:, pl.ds(g, 1), :] = jnp.sum(total, axis=1, keepdims=True)

    def order(n):
        both = jnp.minimum(chip, chips - 1 - chip)
        h = (n + 1) // 2
        two_sided = jnp.where(n % 2 == 1, chip - h, chip + h)
        far = n - both
        one_sided = jnp.where(chip <= chips - 1 - chip, chip + far, chip - far)
        return jnp.where(n <= 2 * both, two_sided, one_sided)

    def visit(slot, carry):
        n = slot // (2 * groups_own)
        at = slot % (2 * groups_own)
        gl = at % groups_own
        p = order(n)
        for later in range(1, groups_own):
            pl.when((n > 0) & (at == later))(functools.partial(handle, n, later))
        pl.when((n + 1 < chips) & (at == 2 * groups_own - 1))(functools.partial(handle, n + 1, 0))
        for which in range(groups_own):
            @pl.when(at == groups_own + which)
            def _():
                part_copy(p, which, 1 - core).wait_recv()

        side = jnp.where(at < groups_own, core, 1 - core)
        group_forward(p * 2 + side, gl)
        return carry

    lax.fori_loop(0, 2 * groups_own * chips, visit, 0)

    spread_row = lax.broadcasted_iota(jnp.int32, (targets, LANES), 0)
    spread_lane = lax.broadcasted_iota(jnp.int32, (targets, LANES), 1)
    spread = jnp.where(spread_row % PACK == spread_lane // SIDE, 1.0, 0.0).astype(jnp.float32)
    keep_g = lax.broadcasted_iota(jnp.int32, (groups, targets), 0)
    keep_t = lax.broadcasted_iota(jnp.int32, (groups, targets), 1)
    keep = jnp.where(keep_t // PACK == keep_g, 1.0, 0.0).astype(jnp.float32)
    nt_dims = (((1,), (1,)), ((), ()))
    lane_sums = lax.dot_general(
        ksum[...].reshape(own_s * groups, LANES), spread, nt_dims,
        precision=HIGH, preferred_element_type=jnp.float32,
    ) * (1.0 / (PIXELS * 9.0 ** (LAYERS - 1)))
    picked = jnp.sum(lane_sums.reshape(own_s, groups, targets) * keep[None], axis=1)
    kbuf[me] = picked

    others(lambda t, s: k_copy(t, s).start())

    def take_dual(step, carry):
        dual_arrival(lax.rem(si + step, ns)).wait_recv()
        return carry

    lax.fori_loop(1, ns, take_dual, 0)
    duals = dbuf[...].reshape(ns * dual_ref.shape[0], CLASSES)
    own_duals = dual_ref[pl.ds(ti * own_s, own_s), :]
    gram = lax.dot_general(
        own_duals, duals, nt_dims, precision=HIGH, preferred_element_type=jnp.float32
    )
    onehot = tbuf[:, images].reshape(targets, LANES)[:, :CLASSES]
    offset = lax.dot_general(
        own_duals, onehot, nt_dims, precision=HIGH, preferred_element_type=jnp.float32
    )
    accl[...] = jnp.zeros_like(accl)
    accc[...] = jnp.zeros_like(accc)

    k_all().wait_recv()
    columns = jnp.concatenate([kbuf[d] for d in range(ndev)], axis=0)
    weight = jnp.dot(gram, columns, precision=HIGH, preferred_element_type=jnp.float32) - offset
    wide = (weight[:, None, :] * keep[None]).reshape(own_s * groups, targets)
    wexp[...] = jnp.dot(
        wide, spread, precision=HIGH, preferred_element_type=jnp.float32
    ).reshape(own_s, groups, LANES)

    def block_backward(owner, carry):
        level_terms = [[None] * PACK for _ in range(LAYERS)]
        channel_terms = [[None] * PACK for _ in range(CHANNELS)]

        def add(table, at, k, value):
            table[at][k] = value if table[at][k] is None else table[at][k] + value

        for gl in range(groups_own):
            g = owner * groups_own + gl
            upstream = [jnp.broadcast_to(wexp[:, pl.ds(g, 1), :], (own_s, SUB, LANES))] * PACK
            for layer in range(LAYERS - 1, -1, -1):
                passed = []
                for k in range(PACK):
                    add(level_terms, layer, k, upstream[k] * amp[g, layer, k])
                    passed.append(upstream[k] * ang[g, layer, k])
                upstream = box_sum(passed, mask)
            for channel in range(CHANNELS):
                for k in range(PACK):
                    image = tbuf[owner, (gl * CHANNELS + channel) * PACK + k]
                    add(channel_terms, channel, k, upstream[k] * image[None])
        for layer in range(LAYERS):
            for k in range(PACK):
                accl[layer, k] += level_terms[layer][k]
        for channel in range(CHANNELS):
            for k in range(PACK):
                accc[channel, k] += channel_terms[channel][k]
        return carry

    lax.fori_loop(0, nt, block_backward, 0)

    def over_images(v):
        v = v + pltpu.roll(v, 2 * SIDE, 2)
        return v + pltpu.roll(v, SIDE, 2)

    level_grad = None
    for layer in range(LAYERS - 1, -1, -1):
        scale = 9.0**layer / (2.0 * math.pi * 9.0 ** (LAYERS - 1 - layer))
        term = [
            over_images(accl[layer, k]) * (sroot[layer, 0, k] * scale) for k in range(PACK)
        ]
        if level_grad is not None:
            carried = box_sum(level_grad, mask)
            term = [t + c * (1.0 / 9.0) for t, c in zip(term, carried)]
        level_grad = term
    energy = [v * (2.0 / (9.0 * CHANNELS)) for v in box_sum(level_grad, mask)]
    for channel in range(CHANNELS):
        natural = None
        for k in range(PACK):
            value = over_images(accc[channel, k]) * (1.0 / (CHANNELS * 9.0**LAYERS))
            value = value + srep[channel, k] * energy[k]
            natural = value if natural is None else jnp.where(mask[4] == k, value, natural)
        flat[...] = natural
        for s in range(SUB):
            grad_ref[channel, s] = flat[:, s, :]

    pred[...] = jnp.dot(columns.T, duals, precision=HIGH, preferred_element_type=jnp.float32)
    residual_ref[...] = pred[pl.ds(ti * own_t, own_t), :] - own_onehot[:own_t, :CLASSES]

    for gl in range(groups_own):
        for way in range(2):
            onward = chip + 1 - 2 * way
            for h in range(chips):
                source = chip - (1 - 2 * way) * h

                @pl.when((source >= 0) & (source < chips) & (onward >= 0) & (onward < chips))
                def _():
                    plane_copy(source, gl, way, onward).wait_send()

        for p in range(chips):
            part_copy(p, gl, core).wait_send()

    def drain_dual(step, carry):
        dual_copy(lax.rem(si + step, ns)).wait_send()
        return carry

    lax.fori_loop(1, ns, drain_dual, 0)

    k_all().wait_send()


def shards(nt, ns, target_pool, target_index, target_labels, dual_weights, support_images):
    own_t = target_index.shape[0]
    own_s = support_images.shape[0]
    groups = nt * own_t // PACK
    images = own_t * CHANNELS
    chips = nt // 2
    ndev = nt * ns
    f32 = jnp.float32
    vmem = pl.BlockSpec(memory_space=pltpu.VMEM)
    smem = pl.BlockSpec(memory_space=pltpu.SMEM)
    dma = pltpu.SemaphoreType.DMA
    tile = (SUB, LANES)
    residual, grad = pl.pallas_call(
        functools.partial(kernel, nt, ns, own_t, own_s),
        out_shape=(
            jax.ShapeDtypeStruct((own_t, CLASSES), f32),
            jax.ShapeDtypeStruct((CHANNELS, SUB, own_s, LANES), f32),
        ),
        in_specs=[smem, smem, vmem, vmem, vmem],
        out_specs=(vmem, vmem),
        scratch_shapes=[
            pltpu.VMEM((nt, images + 1) + tile, f32),
            pltpu.VMEM((ns,) + dual_weights.shape, f32),
            pltpu.VMEM((ndev, own_s, nt * own_t), f32),
            pltpu.VMEM((CHANNELS, PACK, own_s) + tile, f32),
            pltpu.VMEM((LAYERS, 2, PACK, own_s) + tile, f32),
            pltpu.VMEM((LAYERS, 2, PACK) + tile, f32),
            pltpu.VMEM((groups, LAYERS, PACK, own_s) + tile, f32),
            pltpu.VMEM((groups, LAYERS, PACK, own_s) + tile, f32),
            pltpu.VMEM((own_s, groups, LANES), f32),
            pltpu.VMEM((own_s, groups, LANES), f32),
            pltpu.VMEM((LAYERS, PACK, own_s) + tile, f32),
            pltpu.VMEM((CHANNELS, PACK, own_s) + tile, f32),
            pltpu.VMEM((nt * own_t, CLASSES), f32),
            pltpu.VMEM((own_s,) + tile, f32),
            dma((2, chips, own_t // PACK)),
            dma((chips, own_t // PACK)),
            dma((chips, own_t // PACK)),
            dma((chips, own_t // PACK)),
            dma((ns,)),
            dma((ns,)),
            dma,
            dma,
        ],
        compiler_params=pltpu.CompilerParams(collective_id=0, has_side_effects=True),
    )(
        target_index,
        target_labels,
        target_pool.reshape(-1, SUB, CHANNELS, SUB, LANES).transpose(2, 0, 3, 1, 4),
        dual_weights,
        support_images.reshape(own_s, CHANNELS, SUB, LANES).transpose(1, 2, 0, 3),
    )
    return (residual, grad.transpose(2, 0, 1, 3).reshape(support_images.shape))


def solution(mesh):
    in_specs = (
        P("tgt", None, None),
        P("tgt"),
        P("tgt"),
        P("sup", None),
        P(("sup", "tgt"), None, None),
    )
    out_specs = (P("tgt", None), P(("sup", "tgt"), None, None))
    body = functools.partial(shards, mesh.shape["tgt"], mesh.shape["sup"])
    return jax.shard_map(body, mesh=mesh, in_specs=in_specs, out_specs=out_specs, check_vma=False)
```

```python
import functools
import math

import jax
import jax.numpy as jnp
from jax import lax
from jax.experimental import pallas as pl
from jax.experimental.pallas import tpu as pltpu
from jax.sharding import PartitionSpec as P

CHANNELS = 3
SIDE = 32
CLASSES = 100
LAYERS = 3
PIXELS = 1024
BETA = 0.01
PACK = 4
SUB = 8
LANES = 128
MESH = pl.DeviceIdType.MESH
HIGH = lax.Precision.HIGHEST
ACOS = (
    1.5707963050,
    -0.2145988016,
    0.0889789874,
    -0.0501743046,
    0.0308918810,
    -0.0170881256,
    0.0066700901,
    -0.0012624911,
)


def masks():
    lane = lax.broadcasted_iota(jnp.int32, (SUB, LANES), 1)
    row = lax.broadcasted_iota(jnp.int32, (SUB, LANES), 0)
    column = lane % SIDE
    return (column > 0, column < SIDE - 1, row > 0, row < SUB - 1, lane // SIDE)


def box_sum(maps, mask):
    right, left, down, up, _ = mask
    axis = maps[0].ndim - 1

    def across(v):
        return (
            v
            + jnp.where(right, pltpu.roll(v, 1, axis), 0.0)
            + jnp.where(left, pltpu.roll(v, LANES - 1, axis), 0.0)
        )

    before = jnp.where(down, pltpu.roll(maps[3], 1, axis - 1), 0.0)
    after = jnp.where(up, pltpu.roll(maps[0], SUB - 1, axis - 1), 0.0)
    low = maps[0] + maps[1]
    high = maps[2] + maps[3]
    return [across(v) for v in (before + low, low + maps[2], maps[1] + high, high + after)]


def interleave(images, mask):
    group = mask[4]
    out = []
    for k in range(PACK):
        total = None
        for m in range(PACK):
            shift = ((m - k) * SIDE) % LANES
            moved = images[m] if shift == 0 else pltpu.roll(images[m], shift, 1)
            total = moved if total is None else jnp.where(group == m, moved, total)
        out.append(total)
    return out


def replicate(image, mask):
    group = mask[4]
    out = []
    rolled = [image] + [pltpu.roll(image, SIDE * s, 1) for s in range(1, PACK)]
    for k in range(PACK):
        total = None
        for m in range(PACK):
            moved = rolled[(m - k) % PACK]
            total = moved if total is None else jnp.where(group == m, moved, total)
        out.append(total)
    return out


def levels_of(images, mask):
    energy = []
    for k in range(PACK):
        total = images[0][k] * images[0][k]
        for channel in range(1, CHANNELS):
            total = total + images[channel][k] * images[channel][k]
        energy.append(total * (1.0 / CHANNELS))
    levels = []
    current = energy
    for _ in range(LAYERS):
        current = [v * (1.0 / 9.0) + BETA for v in box_sum(current, mask)]
        levels.append(current)
    return levels


def kernel(
    nt, ns, own_t, own_s,
    index_ref, label_ref, pool_ref, dual_ref, support_ref,
    residual_ref, grad_ref,
    tbuf, hbuf, dbuf, kbuf, srep, sroot, tlev, amp, ang, ksum, wexp, accl, accc, pred, flat,
    plane_send, plane_recv, sup_send, sup_recv, hot_send, hot_recv, part_send, part_recv, dual_send, dual_recv, k_send, k_recv,
):
    ti = lax.axis_index("tgt")
    si = lax.axis_index("sup")
    chips = nt // 2
    chip = ti // 2
    core = ti % 2
    ndev = nt * ns
    me = si * nt + ti
    groups_own = own_t // PACK
    groups = nt * groups_own
    images = groups_own * CHANNELS * PACK
    targets = nt * own_t
    mask = masks()

    barrier = pltpu.get_barrier_semaphore()

    def others(action):
        for s in range(ns):
            for t in range(nt):
                pl.when((si != s) | (ti != t))(functools.partial(action, t, s))

    def greet(t, s):
        pl.semaphore_signal(barrier, inc=1, device_id=(t, s), device_id_type=MESH)

    others(greet)

    pool = pool_ref.shape[1] * SUB
    picks = [lax.rem(index_ref[t], pool) for t in range(own_t)]
    for gl in range(groups_own):
        for channel in range(CHANNELS):
            natural = [
                pool_ref[channel, at // SUB, :, pl.ds(at % SUB, 1), :].reshape(SUB, LANES)
                for at in picks[gl * PACK : (gl + 1) * PACK]
            ]
            phases = interleave(natural, mask)
            for k in range(PACK):
                tbuf[ti, (gl * CHANNELS + channel) * PACK + k] = phases[k]
    row = lax.broadcasted_iota(jnp.int32, (SUB, LANES), 0)
    lane = lax.broadcasted_iota(jnp.int32, (SUB, LANES), 1)
    label = jnp.zeros((SUB, LANES), jnp.int32)
    for r in range(own_t):
        label = jnp.where(row == r, label_ref[r], label)
    own_onehot = jnp.where(label == lane, 1.0, 0.0).astype(jnp.float32)
    hbuf[ti] = own_onehot
    dbuf[si] = dual_ref[...]

    pl.semaphore_wait(barrier, ndev - 1)

    size = images // ns

    def order(n):
        both = jnp.minimum(chip, chips - 1 - chip)
        h = (n + 1) // 2
        two_sided = jnp.where(n % 2 == 1, chip - h, chip + h)
        far = n - both
        one_sided = jnp.where(chip <= chips - 1 - chip, chip + far, chip - far)
        return jnp.where(n <= 2 * both, two_sided, one_sided)

    def piece_copy(owner, j, send_sem, recv_sem, device):
        piece = tbuf.at[owner, pl.ds(j * size, size)]
        return pltpu.make_async_remote_copy(
            src_ref=piece,
            dst_ref=piece,
            send_sem=send_sem,
            recv_sem=recv_sem,
            device_id=device,
            device_id_type=MESH,
        )

    def plane_copy(source, target):
        return piece_copy(
            source * 2 + core, si, plane_send.at[target], plane_recv.at[source],
            (target * 2 + core, si),
        )

    def sup_copy(p, j, s):
        return piece_copy(p * 2 + core, j, sup_send.at[p, s], sup_recv.at[p, j], (ti, s))

    def part_copy(p, j, side):
        return piece_copy(
            p * 2 + side, j, part_send.at[p, j], part_recv.at[p, j], (chip * 2 + 1 - core, si)
        )

    def hot_copy(t):
        return pltpu.make_async_remote_copy(
            src_ref=hbuf.at[ti],
            dst_ref=hbuf.at[ti],
            send_sem=hot_send,
            recv_sem=hot_recv,
            device_id=(t, si),
            device_id_type=MESH,
        )

    def hot_all():
        return pltpu.make_async_remote_copy(
            src_ref=hbuf.at[pl.ds(0, nt - 1)],
            dst_ref=hbuf.at[pl.ds(0, nt - 1)],
            send_sem=hot_send,
            recv_sem=hot_recv,
            device_id=(chip * 2 + 1 - core, si),
            device_id_type=MESH,
        )

    def spread_own_piece(m):
        p = order(m)
        plane_copy(p, p).wait_recv()
        for step in range(1, ns):
            sup_copy(p, si, lax.rem(si + step, ns)).start()
        part_copy(p, si, core).start()

    def collect_pieces(m):
        p = order(m)
        for step in range(1, ns):
            j = lax.rem(si + step, ns)
            sup_copy(p, j, j).wait_recv()
            part_copy(p, j, core).start()

    def dual_copy(s):
        return pltpu.make_async_remote_copy(
            src_ref=dbuf.at[si],
            dst_ref=dbuf.at[si],
            send_sem=dual_send.at[s],
            recv_sem=dual_recv.at[si],
            device_id=(ti, s),
            device_id_type=MESH,
        )

    def dual_arrival(s):
        return pltpu.make_async_remote_copy(
            src_ref=dbuf.at[s],
            dst_ref=dbuf.at[s],
            send_sem=dual_send.at[s],
            recv_sem=dual_recv.at[s],
            device_id=(ti, s),
            device_id_type=MESH,
        )

    def k_copy(t, s):
        return pltpu.make_async_remote_copy(
            src_ref=kbuf.at[me],
            dst_ref=kbuf.at[me],
            send_sem=k_send,
            recv_sem=k_recv,
            device_id=(t, s),
            device_id_type=MESH,
        )

    def k_all():
        others_slots = kbuf.at[pl.ds(0, ndev - 1)]
        return pltpu.make_async_remote_copy(
            src_ref=others_slots,
            dst_ref=others_slots,
            send_sem=k_send,
            recv_sem=k_recv,
            device_id=(1 - core + chip * 2, si),
            device_id_type=MESH,
        )

    for h in range(1, chips):
        for target in (chip - h, chip + h):
            @pl.when((target >= 0) & (target < chips))
            def _():
                plane_copy(chip, target).start()

    for j in range(ns):
        part_copy(chip, j, core).start()
    for t in range(nt):
        pl.when(ti != t)(lambda t=t: hot_copy(t).start())

    def send_dual(step, carry):
        dual_copy(lax.rem(si + step, ns)).start()
        return carry

    lax.fori_loop(1, ns, send_dual, 0)

    for m in range(own_s):
        reps = []
        for channel in range(CHANNELS):
            phases = replicate(support_ref[channel, :, m, :], mask)
            reps.append(phases)
            for k in range(PACK):
                srep[channel, k, m] = phases[k]
        levels = levels_of(reps, mask)
        for layer in range(LAYERS):
            for k in range(PACK):
                inverse = lax.rsqrt(levels[layer][k])
                sroot[layer, 0, k, m] = inverse * (1.0 / 9.0**layer)
                sroot[layer, 1, k, m] = levels[layer][k] * inverse * (9.0**layer / math.pi)

    def group_forward(owner, gl):
        g = owner * groups_own + gl
        image = [
            [tbuf[owner, (gl * CHANNELS + channel) * PACK + k] for k in range(PACK)]
            for channel in range(CHANNELS)
        ]
        levels = levels_of(image, mask)
        for layer in range(LAYERS):
            for k in range(PACK):
                inverse = lax.rsqrt(levels[layer][k])
                tlev[layer, 0, k] = inverse
                tlev[layer, 1, k] = levels[layer][k] * inverse
        current = []
        for k in range(PACK):
            total = image[0][k][None] * srep[0, k]
            for channel in range(1, CHANNELS):
                total = total + image[channel][k][None] * srep[channel, k]
            current.append(total)
        cross = [v * (1.0 / 27.0) + BETA for v in box_sum(current, mask)]
        for layer in range(LAYERS):
            mapped = []
            for k in range(PACK):
                x = cross[k] * (tlev[layer, 0, k][None] * sroot[layer, 0, k])
                size = jnp.abs(x)
                gap = jnp.maximum(1.0 - size, 1e-20)
                rest = 1.0 + size
                half = gap * lax.rsqrt(gap)
                poly = size * (ACOS[7] / math.pi) + ACOS[6] / math.pi
                for term in ACOS[5::-1]:
                    poly = poly * size + term / math.pi
                near = half * poly
                slope = jnp.where(x >= 0.0, 1.0 - near, near)
                sine = half * (rest * lax.rsqrt(rest))
                scaled = sine * tlev[layer, 1, k][None]
                amp[g, layer, k] = scaled
                ang[g, layer, k] = slope
                mapped.append(scaled * sroot[layer, 1, k] + slope * cross[k])
            if layer + 1 < LAYERS:
                cross = [v + BETA * 9.0 ** (layer + 1) for v in box_sum(mapped, mask)]
        total = (mapped[0] + mapped[1]) + (mapped[2] + mapped[3])
        ksum[:, pl.ds(g, 1), :] = jnp.sum(total, axis=1, keepdims=True)

    def visit(slot, carry):
        n = slot // (2 * groups_own)
        at = slot % (2 * groups_own)
        gl = at % groups_own
        p = order(n)
        per = 2 * groups_own
        for m in range(1, chips):
            pl.when(slot == 2 * m + 1)(functools.partial(spread_own_piece, m))
            pl.when(slot == (per if m == 1 else per * m - 1))(functools.partial(collect_pieces, m))

        @pl.when(at == groups_own)
        def _():
            for j in range(ns):
                part_copy(p, j, 1 - core).wait_recv()

        side = jnp.where(at < groups_own, core, 1 - core)
        group_forward(p * 2 + side, gl)
        return carry

    lax.fori_loop(0, 2 * groups_own * chips, visit, 0)

    spread_row = lax.broadcasted_iota(jnp.int32, (targets, LANES), 0)
    spread_lane = lax.broadcasted_iota(jnp.int32, (targets, LANES), 1)
    spread = jnp.where(spread_row % PACK == spread_lane // SIDE, 1.0, 0.0).astype(jnp.float32)
    keep_g = lax.broadcasted_iota(jnp.int32, (groups, targets), 0)
    keep_t = lax.broadcasted_iota(jnp.int32, (groups, targets), 1)
    keep = jnp.where(keep_t // PACK == keep_g, 1.0, 0.0).astype(jnp.float32)
    nt_dims = (((1,), (1,)), ((), ()))
    lane_sums = lax.dot_general(
        ksum[...].reshape(own_s * groups, LANES), spread, nt_dims,
        precision=HIGH, preferred_element_type=jnp.float32,
    ) * (1.0 / (PIXELS * 9.0 ** (LAYERS - 1)))
    picked = jnp.sum(lane_sums.reshape(own_s, groups, targets) * keep[None], axis=1)
    kbuf[me] = picked

    others(lambda t, s: k_copy(t, s).start())

    def take_dual(step, carry):
        dual_arrival(lax.rem(si + step, ns)).wait_recv()
        return carry

    lax.fori_loop(1, ns, take_dual, 0)
    duals = dbuf[...].reshape(ns * dual_ref.shape[0], CLASSES)
    own_duals = dual_ref[pl.ds(ti * own_s, own_s), :]
    gram = lax.dot_general(
        own_duals, duals, nt_dims, precision=HIGH, preferred_element_type=jnp.float32
    )
    hot_all().wait_recv()
    onehot = hbuf[...].reshape(targets, LANES)[:, :CLASSES]
    offset = lax.dot_general(
        own_duals, onehot, nt_dims, precision=HIGH, preferred_element_type=jnp.float32
    )
    accl[...] = jnp.zeros_like(accl)
    accc[...] = jnp.zeros_like(accc)

    k_all().wait_recv()
    columns = jnp.concatenate([kbuf[d] for d in range(ndev)], axis=0)
    weight = jnp.dot(gram, columns, precision=HIGH, preferred_element_type=jnp.float32) - offset
    wide = (weight[:, None, :] * keep[None]).reshape(own_s * groups, targets)
    wexp[...] = jnp.dot(
        wide, spread, precision=HIGH, preferred_element_type=jnp.float32
    ).reshape(own_s, groups, LANES)

    def block_backward(owner, carry):
        level_terms = [[None] * PACK for _ in range(LAYERS)]
        channel_terms = [[None] * PACK for _ in range(CHANNELS)]

        def add(table, at, k, value):
            table[at][k] = value if table[at][k] is None else table[at][k] + value

        for gl in range(groups_own):
            g = owner * groups_own + gl
            upstream = [jnp.broadcast_to(wexp[:, pl.ds(g, 1), :], (own_s, SUB, LANES))] * PACK
            for layer in range(LAYERS - 1, -1, -1):
                passed = []
                for k in range(PACK):
                    add(level_terms, layer, k, upstream[k] * amp[g, layer, k])
                    passed.append(upstream[k] * ang[g, layer, k])
                upstream = box_sum(passed, mask)
            for channel in range(CHANNELS):
                for k in range(PACK):
                    image = tbuf[owner, (gl * CHANNELS + channel) * PACK + k]
                    add(channel_terms, channel, k, upstream[k] * image[None])
        for layer in range(LAYERS):
            for k in range(PACK):
                accl[layer, k] += level_terms[layer][k]
        for channel in range(CHANNELS):
            for k in range(PACK):
                accc[channel, k] += channel_terms[channel][k]
        return carry

    lax.fori_loop(0, nt, block_backward, 0)

    def over_images(v):
        v = v + pltpu.roll(v, 2 * SIDE, 2)
        return v + pltpu.roll(v, SIDE, 2)

    level_grad = None
    for layer in range(LAYERS - 1, -1, -1):
        scale = 9.0**layer / (2.0 * math.pi * 9.0 ** (LAYERS - 1 - layer))
        term = [
            over_images(accl[layer, k]) * (sroot[layer, 0, k] * scale) for k in range(PACK)
        ]
        if level_grad is not None:
            carried = box_sum(level_grad, mask)
            term = [t + c * (1.0 / 9.0) for t, c in zip(term, carried)]
        level_grad = term
    energy = [v * (2.0 / (9.0 * CHANNELS)) for v in box_sum(level_grad, mask)]
    for channel in range(CHANNELS):
        natural = None
        for k in range(PACK):
            value = over_images(accc[channel, k]) * (1.0 / (CHANNELS * 9.0**LAYERS))
            value = value + srep[channel, k] * energy[k]
            natural = value if natural is None else jnp.where(mask[4] == k, value, natural)
        flat[...] = natural
        for s in range(SUB):
            grad_ref[channel, s] = flat[:, s, :]

    pred[...] = jnp.dot(columns.T, duals, precision=HIGH, preferred_element_type=jnp.float32)
    residual_ref[...] = pred[pl.ds(ti * own_t, own_t), :] - own_onehot[:own_t, :CLASSES]

    for p in range(chips):
        @pl.when(chip != p)
        def _():
            plane_copy(chip, p).wait_send()
            for step in range(1, ns):
                sup_copy(p, si, lax.rem(si + step, ns)).wait_send()

        for j in range(ns):
            part_copy(p, j, core).wait_send()

    hot_all().wait_send()

    def drain_dual(step, carry):
        dual_copy(lax.rem(si + step, ns)).wait_send()
        return carry

    lax.fori_loop(1, ns, drain_dual, 0)

    k_all().wait_send()


def shards(nt, ns, target_pool, target_index, target_labels, dual_weights, support_images):
    own_t = target_index.shape[0]
    own_s = support_images.shape[0]
    groups = nt * own_t // PACK
    images = own_t * CHANNELS
    chips = nt // 2
    ndev = nt * ns
    f32 = jnp.float32
    vmem = pl.BlockSpec(memory_space=pltpu.VMEM)
    smem = pl.BlockSpec(memory_space=pltpu.SMEM)
    dma = pltpu.SemaphoreType.DMA
    tile = (SUB, LANES)
    residual, grad = pl.pallas_call(
        functools.partial(kernel, nt, ns, own_t, own_s),
        out_shape=(
            jax.ShapeDtypeStruct((own_t, CLASSES), f32),
            jax.ShapeDtypeStruct((CHANNELS, SUB, own_s, LANES), f32),
        ),
        in_specs=[smem, smem, vmem, vmem, vmem],
        out_specs=(vmem, vmem),
        scratch_shapes=[
            pltpu.VMEM((nt, images) + tile, f32),
            pltpu.VMEM((nt,) + tile, f32),
            pltpu.VMEM((ns,) + dual_weights.shape, f32),
            pltpu.VMEM((ndev, own_s, nt * own_t), f32),
            pltpu.VMEM((CHANNELS, PACK, own_s) + tile, f32),
            pltpu.VMEM((LAYERS, 2, PACK, own_s) + tile, f32),
            pltpu.VMEM((LAYERS, 2, PACK) + tile, f32),
            pltpu.VMEM((groups, LAYERS, PACK, own_s) + tile, f32),
            pltpu.VMEM((groups, LAYERS, PACK, own_s) + tile, f32),
            pltpu.VMEM((own_s, groups, LANES), f32),
            pltpu.VMEM((own_s, groups, LANES), f32),
            pltpu.VMEM((LAYERS, PACK, own_s) + tile, f32),
            pltpu.VMEM((CHANNELS, PACK, own_s) + tile, f32),
            pltpu.VMEM((nt * own_t, CLASSES), f32),
            pltpu.VMEM((own_s,) + tile, f32),
            dma((chips,)),
            dma((chips,)),
            dma((chips, ns)),
            dma((chips, ns)),
            dma,
            dma,
            dma((chips, ns)),
            dma((chips, ns)),
            dma((ns,)),
            dma((ns,)),
            dma,
            dma,
        ],
        compiler_params=pltpu.CompilerParams(collective_id=0, has_side_effects=True),
    )(
        target_index,
        target_labels,
        target_pool.reshape(-1, SUB, CHANNELS, SUB, LANES).transpose(2, 0, 3, 1, 4),
        dual_weights,
        support_images.reshape(own_s, CHANNELS, SUB, LANES).transpose(1, 2, 0, 3),
    )
    return (residual, grad.transpose(2, 0, 1, 3).reshape(support_images.shape))


def solution(mesh):
    in_specs = (
        P("tgt", None, None),
        P("tgt"),
        P("tgt"),
        P("sup", None),
        P(("sup", "tgt"), None, None),
    )
    out_specs = (P("tgt", None), P(("sup", "tgt"), None, None))
    body = functools.partial(shards, mesh.shape["tgt"], mesh.shape["sup"])
    return jax.shard_map(body, mesh=mesh, in_specs=in_specs, out_specs=out_specs, check_vma=False)
```
